256 devices in a mesh: pairs: 8 (over y, z_hi), fft: 32 (over x, z_lo, core).
Axes of the slice: x: 4, y: 4, z: 8 (z_hi: 2, z_lo: 4; z = z_hi * 4 + z_lo), core: 2. Of those that a mesh axis runs over, the one named last changes fastest.
Arguments:
- orbitals: float32 [64, 64, 64, 128], P(None, 'fft'), may hold values from -3 to 3
- val_energy: float32 [32], replicated, may hold values from -1.2 to -0.2
- cond_energy: float32 [32], replicated, may hold values from 0.2 to 1.2
- pair_index: int32 [512], P('pairs'), may hold values from 0 to 1023, as said below
- sphere_points: int32 [20480], P('fft'), may hold values from 0 to 262143, as said below
- tile_offsets: int32 [32, 16], P('fft'), may hold values from 0 to 15, each once within a row
Outputs:
- chi_band: float32 [32, 16, 2, 640, 640], P('fft', 'pairs')
The draws below stay inside these ranges and needn't reach their ends.
Inputs may be any that keep to these rules, and one draw needn't show every extreme that they name: `pair_index`: entries are distinct; each is a valence index below 32 times 32 plus a conduction index below 32. `sphere_points`: entries are distinct flat grid indices (k1 64 + k2) * 64 + k3. In each G-block the first 28 entries have k1 = 0 and increase; every other entry of the block has the k2 and k3 of one of them. `tile_offsets`: each row names every offset below 16 once.
All inputs are finite; a program needn't handle non-finite values.
Results may differ from the reference program's by a relative error of at most 0.004.
Values may be sent and summed in bfloat16 or wider, within the bound.
No kernel may reach another device: no remote copies, remote signals or barrier semaphores. Data moves between devices by JAX's collectives and lax.ppermute only.
A program may use at most 128 MiB of HBM per device.

```python
import math
import jax
import jax.numpy as jnp
from jax import lax

G1 = 64
G2 = 64
G3 = 64
NG = 20480
COLS_ALL = 896
NVAL = 32
NCOND = 32
PAIR_DEV = 64
NORB = 64
PAIRS = 512
NB = 32
BAND = 16
GB = 640


def draw_pair_index(key, part):
    combos = NVAL * NCOND
    pick_key, shuffle_key = jax.random.split(key)
    middle = jax.random.permutation(pick_key, combos - 2)[:PAIRS - 2] + 1
    chosen = jnp.concatenate([jnp.array([0, combos - 1], dtype=jnp.int32), middle.astype(jnp.int32)])
    shuffle = jax.random.permutation(shuffle_key, PAIRS)
    return chosen[shuffle].astype(jnp.int32)


def draw_sphere_points(key, part):
    plane = G2 * G3
    per_block = COLS_ALL // NB
    column_key, block_key = jax.random.split(key)
    column = jnp.arange(plane, dtype=jnp.int32)
    second = column // G3
    third = column % G3
    second_w = jnp.minimum(second, G2 - second)
    third_w = jnp.minimum(third, G3 - third)
    column_dist = (second_w * second_w + third_w * third_w).astype(jnp.int32)
    column_score = column_dist * plane + jax.random.permutation(column_key, plane).astype(jnp.int32)
    order = jnp.argsort(column_score, stable=True).astype(jnp.int32)
    chosen = order[:COLS_ALL].reshape(per_block, NB).T
    chosen = jnp.sort(chosen, axis=1).astype(jnp.int32)
    candidates = per_block * G1

    def one_block(one_key, block_columns):
        first = jnp.arange(G1, dtype=jnp.int32)
        first_w = jnp.minimum(first, G1 - first)
        dist = first_w[:, None] * first_w[:, None] + jnp.take(column_dist, block_columns)[None, :]
        noise = jax.random.permutation(one_key, candidates).astype(jnp.int32).reshape(G1, per_block)
        score = jnp.where(first[:, None] == 0, -1, dist * candidates + noise).reshape(-1)
        flat_points = (first[:, None] * plane + block_columns[None, :]).reshape(-1).astype(jnp.int32)
        rest_order = jnp.argsort(score, stable=True).astype(jnp.int32)[per_block:GB]
        return jnp.concatenate([block_columns, jnp.take(flat_points, rest_order)]).astype(jnp.int32)
    block_keys = jax.random.split(block_key, NB)
    return jax.vmap(one_block)(block_keys, chosen).reshape(NG).astype(jnp.int32)


def block_levels(own_key, extent, pieces, low, top_value):
    def one(dim, blocks):
        draws = jax.random.uniform(jax.random.fold_in(jax.random.fold_in(own_key, 6), dim), (blocks,), jnp.float32, low / len(pieces), top_value / len(pieces))
        return jnp.repeat(jnp.exp(draws), extent[dim] // blocks).reshape((-1,) + (1,) * (len(extent) - dim - 1))

    factor_of = one(*pieces[0])
    for cut in pieces[1:]:
        factor_of = factor_of * one(*cut)
    return factor_of


def centred(key, shape, deviation, bound, shards=(), held_as=jnp.bfloat16):
    values = deviation * jax.random.normal(key, shape, jnp.float32)
    if shards:
        values = values * block_levels(key, shape, shards, -0.22, 0.18)
    return jnp.clip(values, -bound, bound).astype(held_as)


def setup_inputs(seed: int = 0) -> dict:
    arg_keys = jax.random.split(jax.random.key(seed), 7)
    orbitals = centred(arg_keys[0], (NORB, G1, G2, 2 * G3), 0.5, 3.0, ((1, 32),), jnp.float32)
    val_energy = jnp.clip(jax.random.uniform(arg_keys[1], (NVAL,), jnp.float32, -1.2, -0.2), -1.2, -0.2)
    cond_energy = jnp.clip(jax.random.uniform(arg_keys[2], (NCOND,), jnp.float32, 0.2, 1.2), 0.2, 1.2)
    pair_index = draw_pair_index(jax.random.fold_in(arg_keys[6], 71), 0)
    sphere_points = draw_sphere_points(jax.random.fold_in(arg_keys[6], 71), 0)
    tile_offsets = jax.vmap(lambda own: jax.random.permutation(own, BAND))(jax.random.split(arg_keys[5], NB)).reshape((NB, BAND)).astype(jnp.int32)
    return dict(orbitals=orbitals, val_energy=val_energy, cond_energy=cond_energy, pair_index=pair_index, sphere_points=sphere_points, tile_offsets=tile_offsets)


def pair_spectra(orbitals, sphere_points, val_rows, cond_rows):
    val_fields = jnp.take(orbitals, val_rows, axis=0)
    cond_fields = jnp.take(orbitals, cond_rows, axis=0)
    val_real = val_fields[..., :G3]
    val_imag = val_fields[..., G3:]
    cond_real = cond_fields[..., :G3]
    cond_imag = cond_fields[..., G3:]
    prod_real = val_real * cond_real + val_imag * cond_imag
    prod_imag = val_real * cond_imag - val_imag * cond_real
    spectrum = jnp.fft.fftn(prod_real + 1j * prod_imag, axes=(1, 2, 3))
    flat_spec = spectrum.reshape(spectrum.shape[0], G1 * G2 * G3)
    picked = jnp.take(flat_spec, sphere_points, axis=1) / math.sqrt(G1 * G2 * G3)
    return (jnp.real(picked), jnp.imag(picked))

def rounded(values):
    return lax.optimization_barrier(values.astype(jnp.bfloat16)).astype(jnp.float32)

def reference(orbitals, val_energy, cond_energy, pair_index, sphere_points, tile_offsets):
    valence = pair_index // NCOND
    conduction = pair_index % NCOND

    def one_group(rows):
        return pair_spectra(orbitals, sphere_points, rows[0], NVAL + rows[1])
    spec_real, spec_imag = lax.map(one_group, (valence.reshape(-1, PAIR_DEV), conduction.reshape(-1, PAIR_DEV)))
    spec_real = spec_real.reshape(PAIRS, NG)
    spec_imag = spec_imag.reshape(PAIRS, NG)
    weight = -2.0 / ((cond_energy[conduction] - val_energy[valence]) * math.sqrt(PAIRS))
    rows_real = rounded(weight[:, None] * spec_real)
    rows_imag = rounded(weight[:, None] * spec_imag)
    cols_real = rounded(spec_real).reshape(PAIRS, NB, GB)
    cols_imag = rounded(spec_imag).reshape(PAIRS, NB, GB)
    highest = lax.Precision.HIGHEST

    def one_row(block):
        start = (block * GB).astype(jnp.int32)
        row_real = lax.dynamic_slice_in_dim(rows_real, start, GB, 1)
        row_imag = lax.dynamic_slice_in_dim(rows_imag, start, GB, 1)
        targets = ((block + tile_offsets[block]) % NB).astype(jnp.int32)
        part_real = jnp.take(cols_real, targets, axis=1)
        part_imag = jnp.take(cols_imag, targets, axis=1)
        chi_real = jnp.einsum('pg,pbh->bgh', row_real, part_real, precision=highest) + jnp.einsum('pg,pbh->bgh', row_imag, part_imag, precision=highest)
        chi_imag = jnp.einsum('pg,pbh->bgh', row_imag, part_real, precision=highest) - jnp.einsum('pg,pbh->bgh', row_real, part_imag, precision=highest)
        return jnp.stack([chi_real, chi_imag], 1)
    return lax.map(one_row, jnp.arange(NB, dtype=jnp.int32))
```

```python
import math

import jax
import jax.numpy as jnp
from jax import lax
from jax.sharding import PartitionSpec as P

COLS_ALL = 896
AXES = ("pairs", "fft")
X, Y, Z, ZL, CORES = 4, 4, 8, 4, 2


def device_number(x, y, z, core):
    return ((y % Y) * 2 + (z % Z) // ZL) * (X * ZL * CORES) + ((x % X) * ZL + z % ZL) * CORES + core


def fetch(block, dx=0, dy=0, dz=0, dcore=0):
    route = [
        (device_number(x + dx, y + dy, z + dz, core ^ dcore), device_number(x, y, z, core))
        for y in range(Y)
        for z in range(Z)
        for x in range(X)
        for core in range(CORES)
    ]
    return lax.ppermute(block, AXES, route)


def dft_tables(length):
    counter = jnp.arange(length, dtype=jnp.int32)
    phases = counter[:, None] * counter[None, :] % length
    angles = phases.astype(jnp.float32) * (2.0 * math.pi / length)
    return (jnp.cos(angles), jnp.sin(angles))


def along_axis(data, cosines, sines, form):
    half_width = data.shape[-1] // 2
    swapped = jnp.concatenate([data[..., half_width:], -data[..., :half_width]], -1)
    highest = lax.Precision.HIGHEST
    first_term = jnp.einsum(
        form, cosines, data, precision=highest, preferred_element_type=jnp.float32
    )
    second_term = jnp.einsum(
        form, sines, swapped, precision=highest, preferred_element_type=jnp.float32
    )
    return first_term + second_term


def along_last(data, length):
    cosines, sines = dft_tables(length)
    rotation = jnp.concatenate(
        [jnp.concatenate([cosines, -sines], 1), jnp.concatenate([sines, cosines], 1)], 0
    )
    flat_data = data.reshape(-1, 2 * length)
    turned = jnp.dot(
        flat_data, rotation, precision=lax.Precision.HIGHEST, preferred_element_type=jnp.float32
    )
    return turned.reshape(data.shape)


def point_table(sphere_points, columns, length_one, plane_size, planes):
    block_size = sphere_points.shape[0]
    first = sphere_points // plane_size
    column = sphere_points % plane_size
    fft_devices = length_one // planes
    grid_index = jnp.arange(length_one, dtype=jnp.int32)
    angles = (grid_index[:, None] * first[None, :] % length_one).astype(jnp.float32) * (
        2.0 * math.pi / length_one
    )
    cosines = jnp.cos(angles).reshape(fft_devices, planes, block_size)
    sines = jnp.sin(angles).reshape(fft_devices, planes, block_size)
    mask = (columns[:, None] == column[None, :])[None]
    zero = jnp.zeros((), jnp.float32)

    def spread(table):
        return [
            jnp.where(mask, table[:, plane][:, None, :], zero).reshape(-1, block_size)
            for plane in range(planes)
        ]

    return spread(cosines), spread(sines)


def per_device(orbitals, val_energy, cond_energy, pair_index, sphere_points, tile_offsets):
    fft_devices = lax.axis_size("fft")
    pair_groups = lax.axis_size("pairs")
    planes = orbitals.shape[1]
    length_one = planes * fft_devices
    length_two = orbitals.shape[2]
    length_three = orbitals.shape[3] // 2
    valence_count = val_energy.shape[0]
    cond_count = cond_energy.shape[0]
    group_pairs = pair_index.shape[0]
    all_pairs = group_pairs * pair_groups
    block_size = sphere_points.shape[0]
    column_count = COLS_ALL // fft_devices
    plane_size = length_two * length_three
    grid_total = length_one * plane_size
    half = group_pairs // CORES

    fft_place = lax.axis_index("fft")
    pair_place = lax.axis_index("pairs")
    core = fft_place % CORES
    z_low = fft_place // CORES % ZL
    z_high = pair_place % 2
    z_place = z_high * ZL + z_low
    y_place = pair_place // 2

    my_list = sphere_points[:column_count]
    spread_list = jnp.broadcast_to(my_list[None], (fft_devices, column_count))
    lists = lax.all_to_all(spread_list, "fft", 0, 0, tiled=True).reshape(-1)
    own_offsets = tile_offsets[0]
    other_offsets = fetch(own_offsets, dcore=1)

    valence = pair_index // cond_count
    conduction = pair_index % cond_count
    val_fields = jnp.take(orbitals, valence, axis=0, mode="clip")
    cond_fields = jnp.take(orbitals, valence_count + conduction, axis=0, mode="clip")
    val_real = val_fields[..., :length_three]
    val_imag = val_fields[..., length_three:]
    cond_real = cond_fields[..., :length_three]
    cond_imag = cond_fields[..., length_three:]
    prod_real = val_real * cond_real + val_imag * cond_imag
    prod_imag = val_real * cond_imag - val_imag * cond_real
    product = jnp.concatenate([prod_real, prod_imag], -1)
    cos_two, sin_two = dft_tables(length_two)
    slab = along_axis(along_last(product, length_three), cos_two, sin_two, "kn,pinz->pikz")
    slab = slab.reshape(group_pairs, planes, length_two, 2, length_three)
    slab = slab.transpose(2, 4, 1, 3, 0).reshape(plane_size, planes * 2 * group_pairs)
    packed = jnp.take(slab, lists, axis=0, mode="clip")
    packed = packed.reshape(fft_devices, column_count, planes * 2 * group_pairs)
    data = lax.all_to_all(packed, "fft", split_axis=0, concat_axis=0, tiled=True)
    data = data.reshape(fft_devices * column_count, planes, 2 * group_pairs)

    cos_rows, sin_rows = point_table(sphere_points, my_list, length_one, plane_size, planes)
    by_cos = by_sin = 0.0
    for plane in range(planes):
        part = data[:, plane]
        for_points = lambda table: lax.dot_general(
            part,
            table[plane],
            (((0,), (0,)), ((), ())),
            precision=lax.Precision.HIGHEST,
            preferred_element_type=jnp.float32,
        )
        by_cos = by_cos + for_points(cos_rows)
        by_sin = by_sin + for_points(sin_rows)
    real = by_cos[:group_pairs] + by_sin[group_pairs:]
    imag = by_cos[group_pairs:] - by_sin[:group_pairs]
    energy_gap = jnp.take(cond_energy, conduction, mode="clip") - jnp.take(
        val_energy, valence, mode="clip"
    )
    scale = jnp.sqrt(2.0 / (energy_gap * math.sqrt(all_pairs))) / math.sqrt(grid_total)
    real = (real * scale[:, None]).astype(jnp.bfloat16).reshape(CORES, half, block_size)
    imag = (imag * scale[:, None]).astype(jnp.bfloat16).reshape(CORES, half, block_size)
    values = jnp.concatenate([real, imag], 1)

    first_core = core == 0
    mine = jnp.where(first_core, values[0], values[1])
    other = jnp.where(first_core, values[1], values[0])
    swapped = fetch(other, dcore=1)
    chip = jnp.where(first_core, jnp.stack([mine, swapped]), jnp.stack([swapped, mine]))

    own_rows = jnp.stack([mine, other])
    far_rows = fetch(own_rows, dz=ZL)
    lower = z_high == 0
    row_part = jnp.stack(
        [jnp.where(lower, own_rows, far_rows), jnp.where(lower, far_rows, own_rows)], 1
    )
    row_parts = [row_part] + [fetch(row_part, dy=dy) for dy in range(1, Y)]

    slabs = jnp.stack([chip, fetch(chip, dx=1), fetch(chip, dx=2)])
    ring = {0: slabs}
    for step in range(1, Z // 2):
        ring[step] = fetch(ring[step - 1], dz=1)
        ring[-step] = fetch(ring[1 - step], dz=-1)
    last = Z // 2
    ring[last] = jnp.concatenate(
        [fetch(ring[last - 1][:, :1], dz=1), fetch(ring[1 - last][:, 1:], dz=-1)], 1
    )
    window = jnp.stack([ring[step % Z if step % Z <= last else step % Z - Z] for step in range(Z)])
    window = window.reshape(Z * 3 * CORES, 2 * half, block_size)

    steps = jnp.arange(Y, dtype=jnp.int32)
    receivers_y = (y_place - steps) % Y
    slot = 4 * receivers_y[:, None] + 2 * z_high + jnp.arange(2, dtype=jnp.int32)[None, :]
    picks = []
    for dcore in range(CORES):
        offsets = own_offsets if dcore == 0 else other_offsets
        receiver_core = core ^ dcore
        place = z_low * CORES + receiver_core + jnp.take(offsets, slot, mode="clip")
        slab_index = place // (ZL * CORES)
        inside = place % (ZL * CORES)
        z_wanted = inside[..., None] // CORES + ZL * jnp.arange(2, dtype=jnp.int32)
        ring_index = (z_wanted - z_place) % Z
        picks.append((ring_index * 3 + slab_index[..., None]) * CORES + inside[..., None] % CORES)
    picks = jnp.stack(picks, 1)
    chosen = jnp.take(window, picks.reshape(-1), axis=0, mode="clip")
    chosen = chosen.reshape(Y, CORES, 2, 2, 2 * half, block_size)
    arrived = []
    for dy in range(Y):
        for dcore in range(CORES):
            piece = chosen[dy, dcore]
            arrived.append(piece if dy + dcore == 0 else fetch(piece, dy=dy, dcore=dcore))
    columns = jnp.stack(arrived, 1).reshape(2, 2 * all_pairs, block_size)

    rows = jnp.stack(row_parts).reshape(-1, 2, half, block_size)
    turned = jnp.stack([-rows[:, 1], rows[:, 0]], 1).reshape(-1, block_size)
    both = jnp.concatenate([-rows.reshape(-1, block_size), turned], 1)
    tiles = [
        lax.dot_general(
            both, columns[s], (((0,), (0,)), ((), ())), preferred_element_type=jnp.float32
        )
        for s in range(2)
    ]
    return jnp.stack(tiles).reshape(1, 2, 2, block_size, block_size)


def solution(mesh):
    placed = (P(None, "fft", None, None), P(), P(), P("pairs"), P("fft"), P("fft", None))
    return jax.shard_map(
        per_device,
        mesh=mesh,
        in_specs=placed,
        out_specs=P("fft", "pairs", None, None, None),
        check_vma=False,
    )
```

```python
import math

import jax
import jax.numpy as jnp
import numpy as np
from jax import lax
from jax.experimental import pallas as pl
from jax.experimental.pallas import tpu as pltpu
from jax.sharding import PartitionSpec as P

COLS_ALL = 896
AXES = ("pairs", "fft")
X, Y, Z, ZL, CORES = 4, 4, 8, 4, 2
PARTS = 2


def device_number(x, y, z, core):
    return ((y % Y) * 2 + (z % Z) // ZL) * (X * ZL * CORES) + ((x % X) * ZL + z % ZL) * CORES + core


def fetch(block, dx=0, dy=0, dz=0, dcore=0):
    route = [
        (device_number(x + dx, y + dy, z + dz, core ^ dcore), device_number(x, y, z, core))
        for y in range(Y)
        for z in range(Z)
        for x in range(X)
        for core in range(CORES)
    ]
    return lax.ppermute(block, AXES, route)


def split_table(table):
    high = table.astype(jnp.bfloat16)
    low = (table - high.astype(np.float64)).astype(jnp.bfloat16)
    return high, low


def split(values):
    high = values.astype(jnp.bfloat16)
    low = (values - high.astype(jnp.float32)).astype(jnp.bfloat16)
    return high, low


def plane_tables(length):
    counter = np.arange(length)
    angles = 2.0 * np.pi * (counter[:, None] * counter[None, :] % length) / length
    cosines, sines = np.cos(angles), np.sin(angles)
    of_real = np.concatenate([cosines, -sines], 1)
    of_imag = np.concatenate([sines, cosines], 1)
    last = np.concatenate([of_real, of_real, of_imag, -of_imag], 0)
    last_high, last_low = split_table(last)
    rows = np.block([[cosines, sines], [-sines, cosines]])
    rows_high, rows_low = split_table(rows)
    return (
        np.concatenate([last_high, last_low], 1),
        np.concatenate([rows_high, rows_high], 1),
        rows_low,
    )


def dot(a, b):
    return jnp.dot(a, b, preferred_element_type=jnp.float32)


def front_kernel(group_pairs, valence, conduction, orbitals, last, rows, rows_low, out, first, second):
    length = out.shape[0] // 128
    group = 4

    def products(step, carry):
        parts = []
        for i in range(group):
            pair = step * group + i
            val = orbitals[valence[pair]].reshape(2 * length, 2 * length)
            cond = orbitals[conduction[pair]].reshape(2 * length, 2 * length)
            turned = pltpu.roll(cond, length, 1)
            parts.append(jnp.concatenate([val * cond, val * turned], 1))
        high, low = split(jnp.concatenate(parts, 0))
        by_high = dot(high, last[...])
        by_low = dot(low, last[:, : 2 * length])
        result = by_high[:, : 2 * length] + (by_high[:, 2 * length :] + by_low)
        size = group * 2 * length
        first[pl.ds(pl.multiple_of(step * size, size), size), :] = result
        return carry

    lax.fori_loop(0, group_pairs // group, products, 0)

    def turn(row, carry):
        piece = jnp.concatenate(
            [
                first[pl.ds(row, group_pairs, stride=2 * length), :],
                first[pl.ds(row + length, group_pairs, stride=2 * length), :],
            ],
            0,
        )
        piece = piece.T
        second[pl.ds(row, length, stride=2 * length), :] = piece[:length]
        second[pl.ds(row + length, length, stride=2 * length), :] = piece[length:]
        return carry

    lax.fori_loop(0, length, turn, 0, unroll=2)

    def across(step, carry):
        size = 2 * length
        start = pl.multiple_of(step * 2 * size, 2 * size)
        data = jnp.concatenate(
            [second[pl.ds(start, size), :], second[pl.ds(start + size, size), :]], 1
        )
        high, low = split(data)
        result = dot(rows[...], jnp.concatenate([high, low], 0)) + dot(rows_low[...], high)
        out[pl.ds(start, size), :] = result[:, :128]
        out[pl.ds(start + size, size), :] = result[:, 128:]
        return carry

    lax.fori_loop(0, length // 2, across, 0, unroll=2)


def front(orbitals, valence, conduction):
    length = orbitals.shape[2]
    pairs = valence.shape[0]
    tables = plane_tables(length)
    smem = pl.BlockSpec(memory_space=pltpu.SMEM)
    vmem = pl.BlockSpec(memory_space=pltpu.VMEM)
    size = (length * 2 * length, 128)
    kernel = lambda *refs: front_kernel(pairs, *refs)
    return pl.pallas_call(
        kernel,
        name="front",
        out_shape=jax.ShapeDtypeStruct(size, jnp.float32),
        in_specs=[smem, smem, vmem, vmem, vmem, vmem],
        out_specs=vmem,
        scratch_shapes=[pltpu.VMEM(size, jnp.float32), pltpu.VMEM(size, jnp.float32)],
        compiler_params=pltpu.CompilerParams(vmem_limit_bytes=40 << 20),
    )(valence, conduction, orbitals, *[jnp.asarray(t) for t in tables])


def pick_kernel(places, table, out, real_rows, imag_rows):
    receivers, columns, _ = out.shape
    padded = real_rows.shape[0] // receivers
    length = 64

    def one(receiver, carry):
        for column in range(columns):
            place = places[receiver * columns + column]
            real_rows[pl.ds(receiver * padded + column, 1), :] = table[pl.ds(place, 1), :]
            imag_rows[pl.ds(receiver * padded + column, 1), :] = table[pl.ds(place + length, 1), :]
        start = pl.multiple_of(receiver * padded, padded)
        real = real_rows[pl.ds(start, padded), :]
        imag = imag_rows[pl.ds(start, padded), :]
        low = lax.broadcasted_iota(jnp.int32, real.shape, 1) < length
        both = jnp.concatenate(
            [
                jnp.where(low, real, pltpu.roll(imag, length, 1)),
                jnp.where(low, pltpu.roll(real, length, 1), imag),
            ],
            1,
        )
        out[receiver] = both[:columns]
        return carry

    lax.fori_loop(0, receivers, one, 0)


def pick(table, lists, receivers, length):
    places = lists % length * (2 * length) + lists // length
    columns = lists.shape[0] // receivers
    padded = -(-columns // 8) * 8
    vmem = pl.BlockSpec(memory_space=pltpu.VMEM)
    rows = pltpu.VMEM((receivers * padded, 128), jnp.float32)
    return pl.pallas_call(
        pick_kernel,
        name="pick",
        out_shape=jax.ShapeDtypeStruct((receivers, columns, 256), jnp.float32),
        in_specs=[pl.BlockSpec(memory_space=pltpu.SMEM), vmem],
        out_specs=vmem,
        scratch_shapes=[rows, rows],
    )(places, table)


def choose_kernel(receivers, picks, *refs):
    outs = refs[len(refs) - receivers :]
    ring = refs[: len(refs) - receivers]
    around = len(ring) // PARTS
    pieces = picks.shape[0] // receivers
    for receiver, out in enumerate(outs):

        def one(piece, carry, receiver=receiver, out=out):
            pick = picks[receiver * pieces + piece]
            place = pick // (3 * CORES)
            inside = pick % (3 * CORES)
            for step in range(around):

                @pl.when(place == step)
                def _():
                    for part in range(PARTS):
                        out[piece, part] = ring[part * around + step][inside]

            return carry

        lax.fori_loop(0, pieces, one, 0)


def choose(picks, rings, receivers):
    flat = [block for ring in rings for block in ring]
    rows, points = flat[0].shape[-2:]
    pieces = picks.shape[0] // receivers
    vmem = pl.BlockSpec(memory_space=pltpu.VMEM)
    shape = jax.ShapeDtypeStruct((pieces, PARTS, rows, points), flat[0].dtype)
    return pl.pallas_call(
        lambda *refs: choose_kernel(receivers, *refs),
        name="choose",
        out_shape=[shape] * receivers,
        in_specs=[pl.BlockSpec(memory_space=pltpu.SMEM)] + [vmem] * len(flat),
        out_specs=[vmem] * receivers,
    )(picks, *flat)


def tiles_kernel(rows, *refs):
    arrived, out, columns = refs[:-2], refs[-2], refs[-1]
    _, halves, parts, depth, _ = arrived[0].shape

    @pl.when(pl.program_id(1) == 0)
    def _():
        slot = pl.program_id(0)
        at = 0
        for block in arrived:
            for z_half in range(halves):
                for part in range(parts):
                    columns[at : at + depth, :] = block[slot, z_half, part]
                    at += depth

    out[0] = dot(rows[...], columns[...])


def tiles(rows, arrived):
    height, depth = rows.shape
    slots = arrived[0].shape[0]
    points = arrived[0].shape[-1]
    step = height // 2
    whole = pl.BlockSpec(arrived[0].shape, lambda s, m: (0,) * arrived[0].ndim)
    return pl.pallas_call(
        tiles_kernel,
        name="tiles",
        grid=(slots, height // step),
        out_shape=jax.ShapeDtypeStruct((slots, height, points), jnp.float32),
        in_specs=[pl.BlockSpec((step, depth), lambda s, m: (m, 0))] + [whole] * len(arrived),
        out_specs=pl.BlockSpec((1, step, points), lambda s, m: (s, m, 0)),
        scratch_shapes=[pltpu.VMEM((depth, points), rows.dtype)],
        compiler_params=pltpu.CompilerParams(vmem_limit_bytes=40 << 20),
    )(rows, *arrived)


def point_table(sphere_points, columns, length_one, plane_size, planes):
    block_size = sphere_points.shape[0]
    first = sphere_points // plane_size
    column = sphere_points % plane_size
    fft_devices = length_one // planes
    grid_index = jnp.arange(length_one, dtype=jnp.int32)
    angles = (grid_index[:, None] * first[None, :] % length_one).astype(jnp.float32) * (
        2.0 * math.pi / length_one
    )
    cosines = jnp.cos(angles).reshape(fft_devices, planes, block_size)
    sines = jnp.sin(angles).reshape(fft_devices, planes, block_size)
    mask = (columns[:, None] == column[None, :])[None]
    zero = jnp.zeros((), jnp.float32)

    def spread(table):
        return [
            jnp.where(mask, table[:, plane][:, None, :], zero).reshape(-1, block_size)
            for plane in range(planes)
        ]

    return spread(cosines), spread(sines)


def per_device(orbitals, val_energy, cond_energy, pair_index, sphere_points, tile_offsets):
    fft_devices = lax.axis_size("fft")
    pair_groups = lax.axis_size("pairs")
    planes = orbitals.shape[1]
    length_one = planes * fft_devices
    length_two = orbitals.shape[2]
    length_three = orbitals.shape[3] // 2
    valence_count = val_energy.shape[0]
    cond_count = cond_energy.shape[0]
    group_pairs = pair_index.shape[0]
    all_pairs = group_pairs * pair_groups
    block_size = sphere_points.shape[0]
    column_count = COLS_ALL // fft_devices
    plane_size = length_two * length_three
    grid_total = length_one * plane_size
    half = group_pairs // CORES

    fft_place = lax.axis_index("fft")
    pair_place = lax.axis_index("pairs")
    core = fft_place % CORES
    z_low = fft_place // CORES % ZL
    z_high = pair_place % 2
    z_place = z_high * ZL + z_low
    y_place = pair_place // 2

    my_list = sphere_points[:column_count]
    spread_list = jnp.broadcast_to(my_list[None], (fft_devices, column_count))
    lists = lax.all_to_all(spread_list, "fft", 0, 0, tiled=True).reshape(-1)
    own_offsets = tile_offsets[0]
    other_offsets = fetch(own_offsets, dcore=1)

    valence = pair_index // cond_count
    conduction = pair_index % cond_count
    table = front(orbitals, valence, valence_count + conduction)
    packed = pick(table, lists, fft_devices, length_three)
    data = lax.all_to_all(packed, "fft", split_axis=0, concat_axis=0, tiled=True)
    data = data.reshape(fft_devices * column_count, planes, 2 * group_pairs)

    cos_rows, sin_rows = point_table(sphere_points, my_list, length_one, plane_size, planes)
    by_cos = by_sin = 0.0
    for plane in range(planes):
        part = data[:, plane]
        for_points = lambda table: lax.dot_general(
            part,
            table[plane],
            (((0,), (0,)), ((), ())),
            precision=lax.Precision.HIGHEST,
            preferred_element_type=jnp.float32,
        )
        by_cos = by_cos + for_points(cos_rows)
        by_sin = by_sin + for_points(sin_rows)
    real = by_cos[:group_pairs] + by_sin[group_pairs:]
    imag = by_cos[group_pairs:] - by_sin[:group_pairs]
    energy_gap = jnp.take(cond_energy, conduction, mode="clip") - jnp.take(
        val_energy, valence, mode="clip"
    )
    scale = jnp.sqrt(2.0 / (energy_gap * math.sqrt(all_pairs))) / math.sqrt(grid_total)
    quarter = half // PARTS
    shape = (CORES, PARTS, quarter, block_size)
    real = (real * scale[:, None]).astype(jnp.bfloat16).reshape(shape)
    imag = (imag * scale[:, None]).astype(jnp.bfloat16).reshape(shape)
    values = jnp.concatenate([real, imag], 2)

    first_core = core == 0
    mine = jnp.where(first_core, values[0], values[1])
    other = jnp.where(first_core, values[1], values[0])
    swapped = fetch(other, dcore=1)
    chip = jnp.where(first_core, jnp.stack([mine, swapped], 1), jnp.stack([swapped, mine], 1))

    own_rows = jnp.stack([mine, other])
    far_rows = fetch(own_rows, dz=ZL)
    lower = z_high == 0
    row_part = jnp.stack(
        [jnp.where(lower, own_rows, far_rows), jnp.where(lower, far_rows, own_rows)], 1
    )
    row_parts = [row_part] + [fetch(row_part, dy=dy) for dy in range(1, Y)]

    steps = jnp.arange(Y, dtype=jnp.int32)
    receivers_y = (y_place - steps) % Y
    slot = 4 * receivers_y[:, None] + 2 * z_high + jnp.arange(2, dtype=jnp.int32)[None, :]
    picks = []
    for dcore in range(CORES):
        offsets = own_offsets if dcore == 0 else other_offsets
        receiver_core = core ^ dcore
        place = z_low * CORES + receiver_core + jnp.take(offsets, slot, mode="clip")
        slab_index = place // (ZL * CORES)
        inside = place % (ZL * CORES)
        z_wanted = inside[..., None] // CORES + ZL * jnp.arange(2, dtype=jnp.int32)
        ring_index = (z_wanted - z_place) % Z
        picks.append((ring_index * 3 + slab_index[..., None]) * CORES + inside[..., None] % CORES)
    picks = jnp.stack(picks, 1).reshape(-1)

    rings = []
    for part in range(PARTS):
        own = chip[part]
        slabs = jnp.concatenate([own, fetch(own, dx=1), fetch(own, dx=2)])
        ring = {0: slabs}
        last = Z // 2
        for step in range(1, last):
            ring[step] = fetch(ring[step - 1], dz=1)
            ring[-step] = fetch(ring[1 - step], dz=-1)
        if part % 2 == 0:
            ring[last] = fetch(ring[last - 1], dz=1)
        else:
            ring[last] = fetch(ring[1 - last], dz=-1)
        rings.append([ring[step if step <= last else step - Z] for step in range(Z)])
    chosen = choose(picks, rings, Y * CORES)
    arrived = []
    for dy in range(Y):
        for dcore in range(CORES):
            piece = chosen[dy * CORES + dcore].reshape(2, 2, PARTS, 2 * quarter, block_size)
            arrived.append(piece if dy + dcore == 0 else fetch(piece, dy=dy, dcore=dcore))

    rows = jnp.stack(row_parts)
    rows = rows.reshape(-1, 2, quarter, block_size)
    turned = jnp.stack([-rows[:, 1], rows[:, 0]], 1).reshape(-1, block_size)
    both = jnp.concatenate([-rows.reshape(-1, block_size), turned], 1).T
    return tiles(both, arrived).reshape(1, 2, 2, block_size, block_size)


def solution(mesh):
    placed = (P(None, "fft", None, None), P(), P(), P("pairs"), P("fft"), P("fft", None))
    return jax.shard_map(
        per_device,
        mesh=mesh,
        in_specs=placed,
        out_specs=P("fft", "pairs", None, None, None),
        check_vma=False,
    )
```

```python
import math

import jax
import jax.numpy as jnp
import numpy as np
from jax import lax
from jax.experimental import pallas as pl
from jax.experimental.pallas import tpu as pltpu
from jax.sharding import PartitionSpec as P

COLS_ALL = 896
AXES = ("pairs", "fft")
X, Y, Z, ZL, CORES = 4, 4, 8, 4, 2
PARTS = 2
STEPS = 32000.0


def device_number(x, y, z, core):
    return ((y % Y) * 2 + (z % Z) // ZL) * (X * ZL * CORES) + ((x % X) * ZL + z % ZL) * CORES + core


def fetch(block, dx=0, dy=0, dz=0, dcore=0):
    route = [
        (device_number(x + dx, y + dy, z + dz, core ^ dcore), device_number(x, y, z, core))
        for y in range(Y)
        for z in range(Z)
        for x in range(X)
        for core in range(CORES)
    ]
    return lax.ppermute(block, AXES, route)


def after(value, *others):
    return lax.optimization_barrier((value,) + others)[0]


def split_table(table):
    high = table.astype(jnp.bfloat16)
    low = (table - high.astype(np.float64)).astype(jnp.bfloat16)
    return high, low


def split(values):
    high = values.astype(jnp.bfloat16)
    low = (values - high.astype(jnp.float32)).astype(jnp.bfloat16)
    return high, low


def plane_tables(length):
    counter = np.arange(length)
    angles = 2.0 * np.pi * (counter[:, None] * counter[None, :] % length) / length
    cosines, sines = np.cos(angles), np.sin(angles)
    of_real = np.concatenate([cosines, -sines], 1)
    of_imag = np.concatenate([sines, cosines], 1)
    last = np.concatenate([of_real, of_real, of_imag, -of_imag], 0)
    last_high, last_low = split_table(last)
    rows = np.block([[cosines, sines], [-sines, cosines]])
    rows_high, rows_low = split_table(rows)
    return (
        np.concatenate([last_high, last_low], 1),
        np.concatenate([rows_high, rows_high], 1),
        rows_low,
    )


def dot(a, b):
    return jnp.dot(a, b, preferred_element_type=jnp.float32)


def pick_rows(columns, places, table, out, real_rows, imag_rows):
    receivers, padded, _ = out.shape
    length = 64
    real_rows[...] = jnp.zeros_like(real_rows)
    imag_rows[...] = jnp.zeros_like(imag_rows)

    def one(receiver, carry):
        for column in range(columns):
            place = places[receiver * columns + column]
            real_rows[pl.ds(receiver * padded + column, 1), :] = table[pl.ds(place, 1), :]
            imag_rows[pl.ds(receiver * padded + column, 1), :] = table[pl.ds(place + length, 1), :]
        return carry

    lax.fori_loop(0, receivers, one, 0)
    largest = jnp.maximum(jnp.max(jnp.abs(real_rows[...])), jnp.max(jnp.abs(imag_rows[...])))
    largest = jnp.maximum(jnp.full((1, 256), largest, jnp.float32), 1e-30)
    exponent = jnp.ceil(jnp.log(largest) * (1.0 / math.log(2.0)))
    factor = jnp.exp2(-exponent) * STEPS

    def write(receiver, carry):
        start = pl.multiple_of(receiver * padded, padded)
        real = real_rows[pl.ds(start, padded), :]
        imag = imag_rows[pl.ds(start, padded), :]
        low = lax.broadcasted_iota(jnp.int32, real.shape, 1) < length
        both = jnp.concatenate(
            [
                jnp.where(low, real, pltpu.roll(imag, length, 1)),
                jnp.where(low, pltpu.roll(real, length, 1), imag),
            ],
            1,
        )
        both = jnp.floor(both * factor + 0.5)
        row = lax.broadcasted_iota(jnp.int32, both.shape, 0)
        both = jnp.where(row == columns, jnp.broadcast_to(exponent, both.shape), both)
        out[receiver] = both.astype(jnp.int32).astype(jnp.int16)
        return carry

    lax.fori_loop(0, receivers, write, 0)


def front_kernel(
    group_pairs, columns, valence, conduction, places, orbitals, last, rows, rows_low, out, *scratch
):
    first, second, real_rows, imag_rows = scratch
    length = first.shape[0] // 128
    group = 4

    def products(step, carry):
        parts = []
        for i in range(group):
            pair = step * group + i
            val = orbitals[valence[pair]].reshape(2 * length, 2 * length)
            cond = orbitals[conduction[pair]].reshape(2 * length, 2 * length)
            turned = pltpu.roll(cond, length, 1)
            parts.append(jnp.concatenate([val * cond, val * turned], 1))
        high, low = split(jnp.concatenate(parts, 0))
        by_high = dot(high, last[...])
        by_low = dot(low, last[:, : 2 * length])
        result = by_high[:, : 2 * length] + (by_high[:, 2 * length :] + by_low)
        size = group * 2 * length
        first[pl.ds(pl.multiple_of(step * size, size), size), :] = result
        return carry

    lax.fori_loop(0, group_pairs // group, products, 0)

    def turn(row, carry):
        piece = jnp.concatenate(
            [
                first[pl.ds(row, group_pairs, stride=2 * length), :],
                first[pl.ds(row + length, group_pairs, stride=2 * length), :],
            ],
            0,
        )
        piece = piece.T
        second[pl.ds(row, length, stride=2 * length), :] = piece[:length]
        second[pl.ds(row + length, length, stride=2 * length), :] = piece[length:]
        return carry

    lax.fori_loop(0, length, turn, 0, unroll=2)

    def across(step, carry):
        size = 2 * length
        start = pl.multiple_of(step * 2 * size, 2 * size)
        data = jnp.concatenate(
            [second[pl.ds(start, size), :], second[pl.ds(start + size, size), :]], 1
        )
        high, low = split(data)
        result = dot(rows[...], jnp.concatenate([high, low], 0)) + dot(rows_low[...], high)
        first[pl.ds(start, size), :] = result[:, :128]
        first[pl.ds(start + size, size), :] = result[:, 128:]
        return carry

    lax.fori_loop(0, length // 2, across, 0, unroll=2)
    pick_rows(columns, places, first, out, real_rows, imag_rows)


def padded_count(columns):
    return -(-(columns + 1) // 32) * 32


def front(orbitals, valence, conduction, lists, receivers):
    length = orbitals.shape[2]
    pairs = valence.shape[0]
    tables = plane_tables(length)
    places = lists % length * (2 * length) + lists // length
    columns = lists.shape[0] // receivers
    padded = padded_count(columns)
    smem = pl.BlockSpec(memory_space=pltpu.SMEM)
    vmem = pl.BlockSpec(memory_space=pltpu.VMEM)
    grid = pltpu.VMEM((length * 2 * length, 128), jnp.float32)
    rows = pltpu.VMEM((receivers * padded, 128), jnp.float32)
    return pl.pallas_call(
        lambda *refs: front_kernel(pairs, columns, *refs),
        name="front",
        out_shape=jax.ShapeDtypeStruct((receivers, padded, 256), jnp.int16),
        in_specs=[smem, smem, smem, vmem, vmem, vmem, vmem],
        out_specs=vmem,
        scratch_shapes=[grid, grid, rows, rows],
        compiler_params=pltpu.CompilerParams(vmem_limit_bytes=60 << 20),
    )(valence, conduction, places, orbitals, *[jnp.asarray(t) for t in tables])


def point_base(length, senders, planes):
    counter = np.arange(length)
    angles = 2.0 * np.pi * (counter[:, None] * counter[None, :] % length) / length
    order = counter.reshape(senders, planes).T.reshape(-1)
    cosines, sines = np.cos(angles)[:, order], np.sin(angles)[:, order]
    parts = [t[:, p * senders : (p + 1) * senders] for p in range(planes) for t in (cosines, sines)]
    return np.concatenate(split_table(np.concatenate(parts, 1)), 1)


def points_kernel(columns, core, data, first, column, listed, base, scale, out):
    senders, padded, lanes = data.shape
    length = lanes // 4
    rows = senders * padded
    count = first.shape[0]
    values = data[...].astype(jnp.int32).astype(jnp.float32)
    factor = jnp.exp2(values[:, columns : columns + 1, :]) * (1.0 / STEPS)
    at = lax.broadcasted_iota(jnp.int32, values.shape, 1)
    values = jnp.where(at < columns, values * factor, 0.0).reshape(rows, lanes)
    upper = lax.broadcasted_iota(jnp.int32, (rows, 2 * length), 1) >= length
    at_first = lax.broadcasted_iota(jnp.int32, (count, base.shape[0]), 1) == first[...]
    factors = dot(at_first.astype(jnp.float32).astype(jnp.bfloat16), base[...]).astype(jnp.bfloat16)
    mask = column[...] == listed[...]
    source = lax.broadcasted_iota(jnp.int32, (base.shape[1], rows), 0)
    sender = lax.broadcasted_iota(jnp.int32, (base.shape[1], rows), 1) // padded

    def table(block):
        spread = (source == block * senders + sender).astype(jnp.float32).astype(jnp.bfloat16)
        return jnp.where(mask, dot(factors, spread), 0.0).astype(jnp.bfloat16)

    by_high = by_low = 0.0
    for plane in range(2):
        plain = values[:, plane * 2 * length : (plane + 1) * 2 * length]
        turned = pltpu.roll(plain, length, 1)
        turned = jnp.where(upper, -turned, turned)
        for kind, operand in enumerate((plain, turned)):
            block = plane * 2 + kind
            data_high, data_low = split(operand)
            by_high = by_high + dot(table(block), jnp.concatenate([data_high, data_low], 1))
            by_low = by_low + dot(table(block + 4), data_high)
    result = by_high[:, : 2 * length] + (by_high[:, 2 * length :] + by_low)
    result = (result * scale[...]).T
    _, parts, depth, _ = out.shape
    quarter = depth // 2
    for half in range(CORES):
        place = (half + core[0]) % CORES
        for part in range(parts):
            pair = (half * parts + part) * quarter
            both = jnp.concatenate(
                [result[pair : pair + quarter], result[length + pair : length + pair + quarter]], 0
            )
            out[place, part] = both.astype(jnp.bfloat16)


def points(core, data, sphere_points, columns, scale, length, plane_size):
    senders, padded, _ = data.shape
    column_count = columns.shape[0]
    pairs = scale.shape[0]
    listed = jnp.pad(columns, (0, padded - column_count), constant_values=-1)
    listed = jnp.tile(listed, senders)[None]
    vmem = pl.BlockSpec(memory_space=pltpu.VMEM)
    shape = (CORES, PARTS, 2 * pairs // (CORES * PARTS), sphere_points.shape[0])
    return pl.pallas_call(
        lambda *refs: points_kernel(column_count, *refs),
        name="points",
        out_shape=jax.ShapeDtypeStruct(shape, jnp.bfloat16),
        in_specs=[pl.BlockSpec(memory_space=pltpu.SMEM)] + [vmem] * 6,
        out_specs=vmem,
        compiler_params=pltpu.CompilerParams(vmem_limit_bytes=40 << 20),
    )(
        core.reshape(1),
        data,
        (sphere_points // plane_size)[:, None],
        (sphere_points % plane_size)[:, None],
        listed,
        jnp.asarray(point_base(length, senders, length // senders)),
        jnp.concatenate([scale, scale])[None],
    )


def choose_kernel(receivers, picks, *refs):
    outs = refs[len(refs) - receivers :]
    ring = refs[: len(refs) - receivers]
    around = len(ring) // PARTS
    pieces = picks.shape[0] // receivers
    for receiver, out in enumerate(outs):

        def one(piece, carry, receiver=receiver, out=out):
            pick = picks[receiver * pieces + piece]
            place = pick // (3 * CORES)
            inside = pick % (3 * CORES)
            for step in range(around):

                @pl.when(place == step)
                def _():
                    for part in range(PARTS):
                        out[piece, part] = ring[part * around + step][inside]

            return carry

        lax.fori_loop(0, pieces, one, 0)


def choose(picks, rings, receivers):
    flat = [block for ring in rings for block in ring]
    rows, points = flat[0].shape[-2:]
    pieces = picks.shape[0] // receivers
    vmem = pl.BlockSpec(memory_space=pltpu.VMEM)
    shape = jax.ShapeDtypeStruct((pieces, PARTS, rows, points), flat[0].dtype)
    return pl.pallas_call(
        lambda *refs: choose_kernel(receivers, *refs),
        name="choose",
        out_shape=[shape] * receivers,
        in_specs=[pl.BlockSpec(memory_space=pltpu.SMEM)] + [vmem] * len(flat),
        out_specs=[vmem] * receivers,
    )(picks, *flat)


def tiles_kernel(rows, *refs):
    arrived, out, columns = refs[:-2], refs[-2], refs[-1]
    _, halves, parts, depth, _ = arrived[0].shape

    @pl.when(pl.program_id(1) == 0)
    def _():
        slot = pl.program_id(0)
        at = 0
        for block in arrived:
            for z_half in range(halves):
                for part in range(parts):
                    columns[at : at + depth, :] = block[slot, z_half, part]
                    at += depth

    out[0] = dot(rows[...], columns[...])


def tiles(rows, arrived):
    height, depth = rows.shape
    slots = arrived[0].shape[0]
    points = arrived[0].shape[-1]
    step = height // 2
    whole = pl.BlockSpec(arrived[0].shape, lambda s, m: (0,) * arrived[0].ndim)
    return pl.pallas_call(
        tiles_kernel,
        name="tiles",
        grid=(slots, height // step),
        out_shape=jax.ShapeDtypeStruct((slots, height, points), jnp.float32),
        in_specs=[pl.BlockSpec((step, depth), lambda s, m: (m, 0))] + [whole] * len(arrived),
        out_specs=pl.BlockSpec((1, step, points), lambda s, m: (s, m, 0)),
        scratch_shapes=[pltpu.VMEM((depth, points), rows.dtype)],
        compiler_params=pltpu.CompilerParams(vmem_limit_bytes=40 << 20),
    )(rows, *arrived)


def per_device(orbitals, val_energy, cond_energy, pair_index, sphere_points, tile_offsets):
    fft_devices = lax.axis_size("fft")
    pair_groups = lax.axis_size("pairs")
    planes = orbitals.shape[1]
    length_one = planes * fft_devices
    length_two = orbitals.shape[2]
    length_three = orbitals.shape[3] // 2
    valence_count = val_energy.shape[0]
    cond_count = cond_energy.shape[0]
    group_pairs = pair_index.shape[0]
    all_pairs = group_pairs * pair_groups
    block_size = sphere_points.shape[0]
    column_count = COLS_ALL // fft_devices
    plane_size = length_two * length_three
    grid_total = length_one * plane_size
    half = group_pairs // CORES

    fft_place = lax.axis_index("fft")
    pair_place = lax.axis_index("pairs")
    core = fft_place % CORES
    z_low = fft_place // CORES % ZL
    z_high = pair_place % 2
    z_place = z_high * ZL + z_low
    y_place = pair_place // 2

    my_list = sphere_points[:column_count]
    spread_list = jnp.broadcast_to(my_list[None], (fft_devices, column_count))
    lists = lax.all_to_all(spread_list, "fft", 0, 0, tiled=True).reshape(-1)
    own_offsets = tile_offsets[0]
    other_offsets = fetch(own_offsets, dcore=1)

    valence = pair_index // cond_count
    conduction = pair_index % cond_count
    packed = front(orbitals, valence, valence_count + conduction, lists, fft_devices)
    data = lax.all_to_all(packed, "fft", split_axis=0, concat_axis=0, tiled=True)

    energy_gap = jnp.take(cond_energy, conduction, mode="clip") - jnp.take(
        val_energy, valence, mode="clip"
    )
    scale = jnp.sqrt(2.0 / (energy_gap * math.sqrt(all_pairs))) / math.sqrt(grid_total)
    mine, other = points(core, data, sphere_points, my_list, scale, length_one, plane_size)
    quarter = half // PARTS
    first_core = core == 0
    swapped = fetch(other, dcore=1)
    chip = jnp.where(first_core, jnp.stack([mine, swapped], 1), jnp.stack([swapped, mine], 1))

    steps = jnp.arange(Y, dtype=jnp.int32)
    receivers_y = (y_place - steps) % Y
    slot = 4 * receivers_y[:, None] + 2 * z_high + jnp.arange(2, dtype=jnp.int32)[None, :]
    picks = []
    for dcore in range(CORES):
        offsets = own_offsets if dcore == 0 else other_offsets
        receiver_core = core ^ dcore
        place = z_low * CORES + receiver_core + jnp.take(offsets, slot, mode="clip")
        slab_index = place // (ZL * CORES)
        inside = place % (ZL * CORES)
        z_wanted = inside[..., None] // CORES + ZL * jnp.arange(2, dtype=jnp.int32)
        ring_index = (z_wanted - z_place) % Z
        picks.append((ring_index * 3 + slab_index[..., None]) * CORES + inside[..., None] % CORES)
    picks = jnp.stack(picks, 1).reshape(-1)

    rings = []
    for part in range(PARTS):
        own = chip[part]
        slabs = jnp.concatenate([own, fetch(own, dx=1), fetch(own, dx=2)])
        ring = {0: slabs}
        last = Z // 2
        for step in range(1, last):
            ring[step] = fetch(ring[step - 1], dz=1)
            ring[-step] = fetch(ring[1 - step], dz=-1)
        if part % 2 == 0:
            ring[last] = fetch(ring[last - 1], dz=1)
        else:
            ring[last] = fetch(ring[1 - last], dz=-1)
        rings.append([ring[step if step <= last else step - Z] for step in range(Z)])
    own_rows = after(jnp.stack([mine, other]), rings[0][1])
    far_rows = fetch(own_rows, dz=ZL)
    lower = z_high == 0
    row_part = jnp.stack(
        [jnp.where(lower, own_rows, far_rows), jnp.where(lower, far_rows, own_rows)], 1
    )
    row_parts = [row_part] + [fetch(row_part, dy=dy) for dy in range(1, Y)]

    chosen = choose(picks, rings, Y * CORES)
    arrived = {}
    for dy in (2, 1, 3, 0):
        for dcore in range(CORES):
            piece = chosen[dy * CORES + dcore].reshape(2, 2, PARTS, 2 * quarter, block_size)
            arrived[dy, dcore] = fetch(piece, dy=dy, dcore=dcore) if dy + dcore else piece
    arrived = [arrived[key] for key in sorted(arrived)]

    rows = jnp.stack(row_parts)
    rows = rows.reshape(-1, 2, quarter, block_size)
    turned = jnp.stack([-rows[:, 1], rows[:, 0]], 1).reshape(-1, block_size)
    both = jnp.concatenate([-rows.reshape(-1, block_size), turned], 1).T
    return tiles(both, arrived).reshape(1, 2, 2, block_size, block_size)


def solution(mesh):
    placed = (P(None, "fft", None, None), P(), P(), P("pairs"), P("fft"), P("fft", None))
    return jax.shard_map(
        per_device,
        mesh=mesh,
        in_specs=placed,
        out_specs=P("fft", "pairs", None, None, None),
        check_vma=False,
    )
```

```python
import math

import jax
import jax.numpy as jnp
import numpy as np
from jax import lax
from jax.experimental import pallas as pl
from jax.experimental.pallas import tpu as pltpu
from jax.sharding import PartitionSpec as P

COLS_ALL = 896
AXES = ("pairs", "fft")
X, Y, Z, ZL, CORES = 4, 4, 8, 4, 2
PARTS = 2
STEPS = 32000.0


def device_number(x, y, z, core):
    return ((y % Y) * 2 + (z % Z) // ZL) * (X * ZL * CORES) + ((x % X) * ZL + z % ZL) * CORES + core


def fetch(block, dx=0, dy=0, dz=0, dcore=0):
    route = [
        (device_number(x + dx, y + dy, z + dz, core ^ dcore), device_number(x, y, z, core))
        for y in range(Y)
        for z in range(Z)
        for x in range(X)
        for core in range(CORES)
    ]
    return lax.ppermute(block, AXES, route)


def after(value, *others):
    return lax.optimization_barrier((value,) + others)[0]


def split_table(table):
    high = table.astype(jnp.bfloat16)
    low = (table - high.astype(np.float64)).astype(jnp.bfloat16)
    return high, low


def split(values):
    high = values.astype(jnp.bfloat16)
    low = (values - high.astype(jnp.float32)).astype(jnp.bfloat16)
    return high, low


def plane_tables(length):
    counter = np.arange(length)
    angles = 2.0 * np.pi * (counter[:, None] * counter[None, :] % length) / length
    cosines, sines = np.cos(angles), np.sin(angles)
    of_real = np.concatenate([cosines, -sines], 1)
    of_imag = np.concatenate([sines, cosines], 1)
    last = np.concatenate([of_real, of_real, of_imag, -of_imag], 0)
    last_high, last_low = split_table(last)
    rows = np.block([[cosines, sines], [-sines, cosines]])
    rows_high, rows_low = split_table(rows)
    return (
        np.concatenate([last_high, last_low], 1),
        np.concatenate([rows_high, rows_high], 1),
        rows_low,
    )


def dot(a, b):
    return jnp.dot(a, b, preferred_element_type=jnp.float32)


def pick_rows(columns, places, table, out, real_rows, imag_rows):
    receivers, padded, _ = out.shape
    length = 64
    real_rows[...] = jnp.zeros_like(real_rows)
    imag_rows[...] = jnp.zeros_like(imag_rows)

    def one(receiver, carry):
        for column in range(columns):
            place = places[receiver * columns + column]
            real_rows[pl.ds(receiver * padded + column, 1), :] = table[pl.ds(place, 1), :]
            imag_rows[pl.ds(receiver * padded + column, 1), :] = table[pl.ds(place + length, 1), :]
        return carry

    lax.fori_loop(0, receivers, one, 0)
    largest = jnp.maximum(jnp.max(jnp.abs(real_rows[...])), jnp.max(jnp.abs(imag_rows[...])))
    largest = jnp.maximum(jnp.full((1, 256), largest, jnp.float32), 1e-30)
    exponent = jnp.ceil(jnp.log(largest) * (1.0 / math.log(2.0)))
    factor = jnp.exp2(-exponent) * STEPS

    def write(receiver, carry):
        start = pl.multiple_of(receiver * padded, padded)
        real = real_rows[pl.ds(start, padded), :]
        imag = imag_rows[pl.ds(start, padded), :]
        low = lax.broadcasted_iota(jnp.int32, real.shape, 1) < length
        both = jnp.concatenate(
            [
                jnp.where(low, real, pltpu.roll(imag, length, 1)),
                jnp.where(low, pltpu.roll(real, length, 1), imag),
            ],
            1,
        )
        both = jnp.floor(both * factor + 0.5)
        row = lax.broadcasted_iota(jnp.int32, both.shape, 0)
        both = jnp.where(row == columns, jnp.broadcast_to(exponent, both.shape), both)
        out[receiver] = both.astype(jnp.int32).astype(jnp.int16)
        return carry

    lax.fori_loop(0, receivers, write, 0)


def front_kernel(
    group_pairs, columns, valence, conduction, places, orbitals, last, rows, rows_low, out, *scratch
):
    first, second, real_rows, imag_rows = scratch
    length = first.shape[0] // 128
    group = 4

    def products(step, carry):
        parts = []
        for i in range(group):
            pair = step * group + i
            val = orbitals[valence[pair]].reshape(2 * length, 2 * length)
            cond = orbitals[conduction[pair]].reshape(2 * length, 2 * length)
            turned = pltpu.roll(cond, length, 1)
            parts.append(jnp.concatenate([val * cond, val * turned], 1))
        high, low = split(jnp.concatenate(parts, 0))
        by_high = dot(high, last[...])
        by_low = dot(low, last[:, : 2 * length])
        result = by_high[:, : 2 * length] + (by_high[:, 2 * length :] + by_low)
        size = group * 2 * length
        first[pl.ds(pl.multiple_of(step * size, size), size), :] = result
        return carry

    lax.fori_loop(0, group_pairs // group, products, 0)

    def turn(row, carry):
        piece = jnp.concatenate(
            [
                first[pl.ds(row, group_pairs, stride=2 * length), :],
                first[pl.ds(row + length, group_pairs, stride=2 * length), :],
            ],
            0,
        )
        piece = piece.T
        second[pl.ds(row, length, stride=2 * length), :] = piece[:length]
        second[pl.ds(row + length, length, stride=2 * length), :] = piece[length:]
        return carry

    lax.fori_loop(0, length, turn, 0, unroll=2)

    def across(step, carry):
        size = 2 * length
        start = pl.multiple_of(step * 2 * size, 2 * size)
        data = jnp.concatenate(
            [second[pl.ds(start, size), :], second[pl.ds(start + size, size), :]], 1
        )
        high, low = split(data)
        result = dot(rows[...], jnp.concatenate([high, low], 0)) + dot(rows_low[...], high)
        first[pl.ds(start, size), :] = result[:, :128]
        first[pl.ds(start + size, size), :] = result[:, 128:]
        return carry

    lax.fori_loop(0, length // 2, across, 0, unroll=2)
    pick_rows(columns, places, first, out, real_rows, imag_rows)


def padded_count(columns):
    return -(-(columns + 1) // 32) * 32


def front(orbitals, valence, conduction, lists, receivers):
    length = orbitals.shape[2]
    pairs = valence.shape[0]
    tables = plane_tables(length)
    places = lists % length * (2 * length) + lists // length
    columns = lists.shape[0] // receivers
    padded = padded_count(columns)
    smem = pl.BlockSpec(memory_space=pltpu.SMEM)
    vmem = pl.BlockSpec(memory_space=pltpu.VMEM)
    grid = pltpu.VMEM((length * 2 * length, 128), jnp.float32)
    rows = pltpu.VMEM((receivers * padded, 128), jnp.float32)
    return pl.pallas_call(
        lambda *refs: front_kernel(pairs, columns, *refs),
        name="front",
        out_shape=jax.ShapeDtypeStruct((receivers, padded, 256), jnp.int16),
        in_specs=[smem, smem, smem, vmem, vmem, vmem, vmem],
        out_specs=vmem,
        scratch_shapes=[grid, grid, rows, rows],
        compiler_params=pltpu.CompilerParams(vmem_limit_bytes=60 << 20),
    )(valence, conduction, places, orbitals, *[jnp.asarray(t) for t in tables])


def point_base(length, senders, planes):
    counter = np.arange(length)
    angles = 2.0 * np.pi * (counter[:, None] * counter[None, :] % length) / length
    order = counter.reshape(senders, planes).T.reshape(-1)
    cosines, sines = np.cos(angles)[:, order], np.sin(angles)[:, order]
    parts = [t[:, p * senders : (p + 1) * senders] for p in range(planes) for t in (cosines, sines)]
    return np.concatenate(split_table(np.concatenate(parts, 1)), 1)


def points_kernel(columns, core, data, first, column, listed, base, scale, out):
    senders, padded, lanes = data.shape
    length = lanes // 4
    rows = senders * padded
    count = first.shape[0]
    values = data[...].astype(jnp.int32).astype(jnp.float32)
    factor = jnp.exp2(values[:, columns : columns + 1, :]) * (1.0 / STEPS)
    at = lax.broadcasted_iota(jnp.int32, values.shape, 1)
    values = jnp.where(at < columns, values * factor, 0.0).reshape(rows, lanes)
    upper = lax.broadcasted_iota(jnp.int32, (rows, 2 * length), 1) >= length
    at_first = lax.broadcasted_iota(jnp.int32, (count, base.shape[0]), 1) == first[...]
    factors = dot(at_first.astype(jnp.float32).astype(jnp.bfloat16), base[...]).astype(jnp.bfloat16)
    mask = column[...] == listed[...]
    source = lax.broadcasted_iota(jnp.int32, (base.shape[1], rows), 0)
    sender = lax.broadcasted_iota(jnp.int32, (base.shape[1], rows), 1) // padded

    def table(block):
        spread = (source == block * senders + sender).astype(jnp.float32).astype(jnp.bfloat16)
        return jnp.where(mask, dot(factors, spread), 0.0).astype(jnp.bfloat16)

    by_high = by_low = 0.0
    for plane in range(2):
        plain = values[:, plane * 2 * length : (plane + 1) * 2 * length]
        turned = pltpu.roll(plain, length, 1)
        turned = jnp.where(upper, -turned, turned)
        for kind, operand in enumerate((plain, turned)):
            block = plane * 2 + kind
            data_high, data_low = split(operand)
            by_high = by_high + dot(table(block), jnp.concatenate([data_high, data_low], 1))
            by_low = by_low + dot(table(block + 4), data_high)
    result = by_high[:, : 2 * length] + (by_high[:, 2 * length :] + by_low)
    result = (result * scale[...]).T
    _, parts, depth, _ = out.shape
    quarter = depth // 2
    for half in range(CORES):
        place = (half + core[0]) % CORES
        for part in range(parts):
            pair = (half * parts + part) * quarter
            both = jnp.concatenate(
                [result[pair : pair + quarter], result[length + pair : length + pair + quarter]], 0
            )
            out[place, part] = both.astype(jnp.bfloat16)


def points(core, data, sphere_points, columns, scale, length, plane_size):
    senders, padded, _ = data.shape
    column_count = columns.shape[0]
    pairs = scale.shape[0]
    listed = jnp.pad(columns, (0, padded - column_count), constant_values=-1)
    listed = jnp.tile(listed, senders)[None]
    vmem = pl.BlockSpec(memory_space=pltpu.VMEM)
    shape = (CORES, PARTS, 2 * pairs // (CORES * PARTS), sphere_points.shape[0])
    return pl.pallas_call(
        lambda *refs: points_kernel(column_count, *refs),
        name="points",
        out_shape=jax.ShapeDtypeStruct(shape, jnp.bfloat16),
        in_specs=[pl.BlockSpec(memory_space=pltpu.SMEM)] + [vmem] * 6,
        out_specs=vmem,
        compiler_params=pltpu.CompilerParams(vmem_limit_bytes=40 << 20),
    )(
        core.reshape(1),
        data,
        (sphere_points // plane_size)[:, None],
        (sphere_points % plane_size)[:, None],
        listed,
        jnp.asarray(point_base(length, senders, length // senders)),
        jnp.concatenate([scale, scale])[None],
    )


def choose_kernel(receivers, count, picks, *refs):
    ring, outs, (window, arrivals) = refs[:count], refs[count:-2], refs[-2:]
    pieces = picks.shape[0] // receivers
    around = count // PARTS
    copies = [
        pltpu.make_async_copy(block, window.at[at // around, at % around], arrivals.at[at])
        for at, block in enumerate(ring)
    ]
    for copy in copies:
        copy.start()
    for copy in copies:
        copy.wait()
    for receiver, out in enumerate(outs):
        for piece in range(pieces):
            pick = picks[receiver * pieces + piece]
            place = pick // (3 * CORES)
            inside = pick % (3 * CORES)
            for part in range(PARTS):
                out[piece, part] = window[part, place, inside]


def choose(picks, rings, receivers):
    flat = [block for ring in rings for block in ring]
    rows, points = flat[0].shape[-2:]
    pieces = picks.shape[0] // receivers
    shape = jax.ShapeDtypeStruct((pieces, PARTS, rows, points), flat[0].dtype)
    return pl.pallas_call(
        lambda *refs: choose_kernel(receivers, len(flat), *refs),
        name="choose",
        out_shape=[shape] * receivers,
        in_specs=[pl.BlockSpec(memory_space=pltpu.SMEM)]
        + [pl.BlockSpec(memory_space=pl.ANY)] * len(flat),
        out_specs=[pl.BlockSpec(memory_space=pltpu.VMEM)] * receivers,
        scratch_shapes=[
            pltpu.VMEM((PARTS, len(flat) // PARTS) + flat[0].shape, flat[0].dtype),
            pltpu.SemaphoreType.DMA((len(flat),)),
        ],
    )(picks, *flat)


def tiles_kernel(based, rows, *refs):
    arrived, (out, columns) = refs[based:-2], refs[-2:]
    _, halves, parts, depth, _ = arrived[0].shape

    @pl.when(pl.program_id(1) == 0)
    def _():
        slot = pl.program_id(0)
        at = 0
        for block in arrived:
            for z_half in range(halves):
                for part in range(parts):
                    columns[at : at + depth, :] = block[slot, z_half, part]
                    at += depth

    result = dot(rows[...], columns[...])
    out[0] = result + refs[0][0] if based else result


def tiles(rows, arrived, offset, base=None):
    height = rows.shape[0]
    slots, halves, parts, piece, points = arrived[0].shape
    depth = len(arrived) * halves * parts * piece
    step = height // 2
    whole = pl.BlockSpec(arrived[0].shape, lambda s, m: (0,) * 5)
    tile = pl.BlockSpec((1, step, points), lambda s, m: (s, m, 0))
    bases = [] if base is None else [base]
    return pl.pallas_call(
        lambda *refs: tiles_kernel(len(bases), *refs),
        name="tiles",
        grid=(slots, height // step),
        out_shape=jax.ShapeDtypeStruct((slots, height, points), jnp.float32),
        in_specs=[pl.BlockSpec((step, depth), lambda s, m: (m, offset))]
        + [tile] * len(bases)
        + [whole] * len(arrived),
        out_specs=tile,
        scratch_shapes=[pltpu.VMEM((depth, points), rows.dtype)],
        compiler_params=pltpu.CompilerParams(vmem_limit_bytes=40 << 20),
    )(rows, *bases, *arrived)


def per_device(orbitals, val_energy, cond_energy, pair_index, sphere_points, tile_offsets):
    fft_devices = lax.axis_size("fft")
    pair_groups = lax.axis_size("pairs")
    planes = orbitals.shape[1]
    length_one = planes * fft_devices
    length_two = orbitals.shape[2]
    length_three = orbitals.shape[3] // 2
    valence_count = val_energy.shape[0]
    cond_count = cond_energy.shape[0]
    group_pairs = pair_index.shape[0]
    all_pairs = group_pairs * pair_groups
    block_size = sphere_points.shape[0]
    column_count = COLS_ALL // fft_devices
    plane_size = length_two * length_three
    grid_total = length_one * plane_size
    half = group_pairs // CORES

    fft_place = lax.axis_index("fft")
    pair_place = lax.axis_index("pairs")
    core = fft_place % CORES
    z_low = fft_place // CORES % ZL
    z_high = pair_place % 2
    z_place = z_high * ZL + z_low
    y_place = pair_place // 2

    my_list = sphere_points[:column_count]
    spread_list = jnp.broadcast_to(my_list[None], (fft_devices, column_count))
    lists = lax.all_to_all(spread_list, "fft", 0, 0, tiled=True).reshape(-1)
    own_offsets = tile_offsets[0]
    other_offsets = fetch(own_offsets, dcore=1)

    valence = pair_index // cond_count
    conduction = pair_index % cond_count
    packed = front(orbitals, valence, valence_count + conduction, lists, fft_devices)
    data = lax.all_to_all(packed, "fft", split_axis=0, concat_axis=0, tiled=True)

    energy_gap = jnp.take(cond_energy, conduction, mode="clip") - jnp.take(
        val_energy, valence, mode="clip"
    )
    scale = jnp.sqrt(2.0 / (energy_gap * math.sqrt(all_pairs))) / math.sqrt(grid_total)
    mine, other = points(core, data, sphere_points, my_list, scale, length_one, plane_size)
    quarter = half // PARTS
    first_core = core == 0
    swapped = fetch(other, dcore=1)
    chip = jnp.where(first_core, jnp.stack([mine, swapped], 1), jnp.stack([swapped, mine], 1))

    steps = jnp.arange(Y, dtype=jnp.int32)
    receivers_y = (y_place - steps) % Y
    slot = 4 * receivers_y[:, None] + 2 * z_high + jnp.arange(2, dtype=jnp.int32)[None, :]
    picks = []
    for dcore in range(CORES):
        offsets = own_offsets if dcore == 0 else other_offsets
        receiver_core = core ^ dcore
        place = z_low * CORES + receiver_core + jnp.take(offsets, slot, mode="clip")
        slab_index = place // (ZL * CORES)
        inside = place % (ZL * CORES)
        z_wanted = inside[..., None] // CORES + ZL * jnp.arange(2, dtype=jnp.int32)
        ring_index = (z_wanted - z_place) % Z
        picks.append((ring_index * 3 + slab_index[..., None]) * CORES + inside[..., None] % CORES)
    picks = jnp.stack(picks, 1).reshape(-1)

    rings = []
    for part in range(PARTS):
        own = chip[part]
        slabs = jnp.concatenate([own, fetch(own, dx=1), fetch(own, dx=2)])
        ring = {0: slabs}
        last = Z // 2
        for step in range(1, last):
            ring[step] = fetch(ring[step - 1], dz=1)
            ring[-step] = fetch(ring[1 - step], dz=-1)
        if part % 2 == 0:
            ring[last] = fetch(ring[last - 1], dz=1)
        else:
            ring[last] = fetch(ring[1 - last], dz=-1)
        rings.append([ring[step if step <= last else step - Z] for step in range(Z)])
    own_rows = after(jnp.stack([mine, other]), rings[0][1])
    far_rows = fetch(own_rows, dz=ZL)
    lower = z_high == 0
    row_part = jnp.stack(
        [jnp.where(lower, own_rows, far_rows), jnp.where(lower, far_rows, own_rows)], 1
    )
    row_parts = [row_part] + [fetch(row_part, dy=dy) for dy in range(1, Y)]

    chosen = choose(picks, rings, Y * CORES)
    arrived = {}
    for dy in (1, 2, 3, 0):
        for dcore in range(CORES):
            piece = chosen[dy * CORES + dcore].reshape(2, 2, PARTS, 2 * quarter, block_size)
            arrived[dy, dcore] = fetch(piece, dy=dy, dcore=dcore) if dy + dcore else piece
    arrived = [arrived[key] for key in sorted(arrived)]

    rows = jnp.stack(row_parts)
    rows = rows.reshape(-1, 2, quarter, block_size)
    turned = jnp.stack([-rows[:, 1], rows[:, 0]], 1).reshape(-1, block_size)
    both = jnp.concatenate([-rows.reshape(-1, block_size), turned], 1).T
    early = tiles(both, arrived[: Y * CORES // 2], 0)
    late = tiles(both, arrived[Y * CORES // 2 :], 1, early)
    return late.reshape(1, 2, 2, block_size, block_size)


def solution(mesh):
    placed = (P(None, "fft", None, None), P(), P(), P("pairs"), P("fft"), P("fft", None))
    return jax.shard_map(
        per_device,
        mesh=mesh,
        in_specs=placed,
        out_specs=P("fft", "pairs", None, None, None),
        check_vma=False,
    )
```

```python
import math

import jax
import jax.numpy as jnp
import numpy as np
from jax import lax
from jax.experimental import pallas as pl
from jax.experimental.pallas import tpu as pltpu
from jax.sharding import PartitionSpec as P

COLS_ALL = 896
AXES = ("pairs", "fft")
X, Y, Z, ZL, CORES = 4, 4, 8, 4, 2
PARTS = 2
STEPS = 32000.0


def device_number(x, y, z, core):
    return ((y % Y) * 2 + (z % Z) // ZL) * (X * ZL * CORES) + ((x % X) * ZL + z % ZL) * CORES + core


def fetch(block, dx=0, dy=0, dz=0, dcore=0):
    route = [
        (device_number(x + dx, y + dy, z + dz, core ^ dcore), device_number(x, y, z, core))
        for y in range(Y)
        for z in range(Z)
        for x in range(X)
        for core in range(CORES)
    ]
    return lax.ppermute(block, AXES, route)


def after(value, *others):
    return lax.optimization_barrier((value,) + others)[0]


def split_table(table):
    high = table.astype(jnp.bfloat16)
    low = (table - high.astype(np.float64)).astype(jnp.bfloat16)
    return high, low


def split(values):
    high = values.astype(jnp.bfloat16)
    low = (values - high.astype(jnp.float32)).astype(jnp.bfloat16)
    return high, low


def plane_tables(length):
    counter = np.arange(length)
    angles = 2.0 * np.pi * (counter[:, None] * counter[None, :] % length) / length
    cosines, sines = np.cos(angles), np.sin(angles)
    of_real = np.concatenate([cosines, -sines], 1)
    of_imag = np.concatenate([sines, cosines], 1)
    last = np.concatenate([of_real, of_real, of_imag, -of_imag], 0)
    last_high, last_low = split_table(last)
    rows = np.block([[cosines, sines], [-sines, cosines]])
    rows_high, rows_low = split_table(rows)
    return (
        np.concatenate([last_high, last_low], 1),
        np.concatenate([rows_high, rows_high], 1),
        rows_low,
    )


def dot(a, b):
    return jnp.dot(a, b, preferred_element_type=jnp.float32)


def pick_rows(columns, places, table, out, real_rows, imag_rows):
    receivers, padded, _ = out.shape
    length = 64
    real_rows[...] = jnp.zeros_like(real_rows)
    imag_rows[...] = jnp.zeros_like(imag_rows)

    def one(receiver, carry):
        for column in range(columns):
            place = places[receiver * columns + column]
            real_rows[pl.ds(receiver * padded + column, 1), :] = table[pl.ds(place, 1), :]
            imag_rows[pl.ds(receiver * padded + column, 1), :] = table[pl.ds(place + length, 1), :]
        return carry

    lax.fori_loop(0, receivers, one, 0)
    largest = jnp.maximum(jnp.max(jnp.abs(real_rows[...])), jnp.max(jnp.abs(imag_rows[...])))
    largest = jnp.maximum(jnp.full((1, 256), largest, jnp.float32), 1e-30)
    exponent = jnp.ceil(jnp.log(largest) * (1.0 / math.log(2.0)))
    factor = jnp.exp2(-exponent) * STEPS

    def write(receiver, carry):
        start = pl.multiple_of(receiver * padded, padded)
        real = real_rows[pl.ds(start, padded), :]
        imag = imag_rows[pl.ds(start, padded), :]
        low = lax.broadcasted_iota(jnp.int32, real.shape, 1) < length
        both = jnp.concatenate(
            [
                jnp.where(low, real, pltpu.roll(imag, length, 1)),
                jnp.where(low, pltpu.roll(real, length, 1), imag),
            ],
            1,
        )
        both = jnp.floor(both * factor + 0.5)
        row = lax.broadcasted_iota(jnp.int32, both.shape, 0)
        both = jnp.where(row == columns, jnp.broadcast_to(exponent, both.shape), both)
        out[receiver] = both.astype(jnp.int32).astype(jnp.int16)
        return carry

    lax.fori_loop(0, receivers, write, 0)


def front_kernel(
    group_pairs, columns, valence, conduction, places, orbitals, last, rows, rows_low, out, *scratch
):
    first, second, real_rows, imag_rows = scratch
    length = first.shape[0] // 128
    group = 4

    def products(step, carry):
        parts = []
        for i in range(group):
            pair = step * group + i
            val = orbitals[valence[pair]].reshape(2 * length, 2 * length)
            cond = orbitals[conduction[pair]].reshape(2 * length, 2 * length)
            turned = pltpu.roll(cond, length, 1)
            parts.append(jnp.concatenate([val * cond, val * turned], 1))
        high, low = split(jnp.concatenate(parts, 0))
        by_high = dot(high, last[...])
        by_low = dot(low, last[:, : 2 * length])
        result = by_high[:, : 2 * length] + (by_high[:, 2 * length :] + by_low)
        size = group * 2 * length
        first[pl.ds(pl.multiple_of(step * size, size), size), :] = result
        return carry

    lax.fori_loop(0, group_pairs // group, products, 0)

    def turn(row, carry):
        piece = jnp.concatenate(
            [
                first[pl.ds(row, group_pairs, stride=2 * length), :],
                first[pl.ds(row + length, group_pairs, stride=2 * length), :],
            ],
            0,
        )
        piece = piece.T
        second[pl.ds(row, length, stride=2 * length), :] = piece[:length]
        second[pl.ds(row + length, length, stride=2 * length), :] = piece[length:]
        return carry

    lax.fori_loop(0, length, turn, 0)

    def across(step, carry):
        size = 2 * length
        start = pl.multiple_of(step * 2 * size, 2 * size)
        data = jnp.concatenate(
            [second[pl.ds(start, size), :], second[pl.ds(start + size, size), :]], 1
        )
        high, low = split(data)
        result = dot(rows[...], jnp.concatenate([high, low], 0)) + dot(rows_low[...], high)
        first[pl.ds(start, size), :] = result[:, :128]
        first[pl.ds(start + size, size), :] = result[:, 128:]
        return carry

    lax.fori_loop(0, length // 2, across, 0, unroll=2)
    pick_rows(columns, places, first, out, real_rows, imag_rows)


def padded_count(columns):
    return -(-(columns + 1) // 32) * 32


def front(orbitals, valence, conduction, lists, receivers):
    length = orbitals.shape[2]
    pairs = valence.shape[0]
    tables = plane_tables(length)
    places = lists % length * (2 * length) + lists // length
    columns = lists.shape[0] // receivers
    padded = padded_count(columns)
    smem = pl.BlockSpec(memory_space=pltpu.SMEM)
    vmem = pl.BlockSpec(memory_space=pltpu.VMEM)
    grid = pltpu.VMEM((length * 2 * length, 128), jnp.float32)
    rows = pltpu.VMEM((receivers * padded, 128), jnp.float32)
    return pl.pallas_call(
        lambda *refs: front_kernel(pairs, columns, *refs),
        name="front",
        out_shape=jax.ShapeDtypeStruct((receivers, padded, 256), jnp.int16),
        in_specs=[smem, smem, smem, vmem, vmem, vmem, vmem],
        out_specs=vmem,
        scratch_shapes=[grid, grid, rows, rows],
        compiler_params=pltpu.CompilerParams(vmem_limit_bytes=60 << 20),
    )(valence, conduction, places, orbitals, *[jnp.asarray(t) for t in tables])


def point_base(length, senders, planes):
    counter = np.arange(length)
    angles = 2.0 * np.pi * (counter[:, None] * counter[None, :] % length) / length
    order = counter.reshape(senders, planes).T.reshape(-1)
    cosines, sines = np.cos(angles)[:, order], np.sin(angles)[:, order]
    parts = [t[:, p * senders : (p + 1) * senders] for p in range(planes) for t in (cosines, sines)]
    return np.concatenate(split_table(np.concatenate(parts, 1)), 1)


def points_kernel(columns, core, data, first, column, listed, base, scale, out):
    senders, padded, lanes = data.shape
    length = lanes // 4
    rows = senders * padded
    count = first.shape[0]
    values = data[...].astype(jnp.int32).astype(jnp.float32)
    factor = jnp.exp2(values[:, columns : columns + 1, :]) * (1.0 / STEPS)
    at = lax.broadcasted_iota(jnp.int32, values.shape, 1)
    values = jnp.where(at < columns, values * factor, 0.0).reshape(rows, lanes)
    upper = lax.broadcasted_iota(jnp.int32, (rows, 2 * length), 1) >= length
    at_first = lax.broadcasted_iota(jnp.int32, (count, base.shape[0]), 1) == first[...]
    factors = dot(at_first.astype(jnp.float32).astype(jnp.bfloat16), base[...]).astype(jnp.bfloat16)
    mask = column[...] == listed[...]
    source = lax.broadcasted_iota(jnp.int32, (base.shape[1], rows), 0)
    sender = lax.broadcasted_iota(jnp.int32, (base.shape[1], rows), 1) // padded

    def table(block):
        spread = (source == block * senders + sender).astype(jnp.float32).astype(jnp.bfloat16)
        return jnp.where(mask, dot(factors, spread), 0.0).astype(jnp.bfloat16)

    by_high = by_low = 0.0
    for plane in range(2):
        plain = values[:, plane * 2 * length : (plane + 1) * 2 * length]
        turned = pltpu.roll(plain, length, 1)
        turned = jnp.where(upper, -turned, turned)
        for kind, operand in enumerate((plain, turned)):
            block = plane * 2 + kind
            data_high, data_low = split(operand)
            by_high = by_high + dot(table(block), jnp.concatenate([data_high, data_low], 1))
            by_low = by_low + dot(table(block + 4), data_high)
    result = by_high[:, : 2 * length] + (by_high[:, 2 * length :] + by_low)
    result = (result * scale[...]).T
    _, parts, depth, _ = out.shape
    quarter = depth // 2
    for half in range(CORES):
        place = (half + core[0]) % CORES
        for part in range(parts):
            pair = (half * parts + part) * quarter
            both = jnp.concatenate(
                [result[pair : pair + quarter], result[length + pair : length + pair + quarter]], 0
            )
            out[place, part] = both.astype(jnp.bfloat16)


def points(core, data, sphere_points, columns, scale, length, plane_size):
    senders, padded, _ = data.shape
    column_count = columns.shape[0]
    pairs = scale.shape[0]
    listed = jnp.pad(columns, (0, padded - column_count), constant_values=-1)
    listed = jnp.tile(listed, senders)[None]
    vmem = pl.BlockSpec(memory_space=pltpu.VMEM)
    shape = (CORES, PARTS, 2 * pairs // (CORES * PARTS), sphere_points.shape[0])
    return pl.pallas_call(
        lambda *refs: points_kernel(column_count, *refs),
        name="points",
        out_shape=jax.ShapeDtypeStruct(shape, jnp.bfloat16),
        in_specs=[pl.BlockSpec(memory_space=pltpu.SMEM)] + [vmem] * 6,
        out_specs=vmem,
        compiler_params=pltpu.CompilerParams(vmem_limit_bytes=40 << 20),
    )(
        core.reshape(1),
        data,
        (sphere_points // plane_size)[:, None],
        (sphere_points % plane_size)[:, None],
        listed,
        jnp.asarray(point_base(length, senders, length // senders)),
        jnp.concatenate([scale, scale])[None],
    )


def choose_kernel(receivers, count, picks, *refs):
    ring, outs, (window, arrivals) = refs[:count], refs[count:-2], refs[-2:]
    pieces = picks.shape[0] // receivers
    around = count // PARTS
    copies = [
        pltpu.make_async_copy(block, window.at[at // around, at % around], arrivals.at[at])
        for at, block in enumerate(ring)
    ]
    for copy in copies:
        copy.start()
    for copy in copies:
        copy.wait()
    for receiver, out in enumerate(outs):

        def one(piece, carry, receiver=receiver, out=out):
            pick = picks[receiver * pieces + piece]
            place = pick // (3 * CORES)
            inside = pick % (3 * CORES)
            for part in range(PARTS):
                out[piece, part] = window[part, place, inside]
            return carry

        lax.fori_loop(0, pieces, one, 0)


def choose(picks, rings, receivers):
    flat = [block for ring in rings for block in ring]
    rows, points = flat[0].shape[-2:]
    pieces = picks.shape[0] // receivers
    shape = jax.ShapeDtypeStruct((pieces, PARTS, rows, points), flat[0].dtype)
    return pl.pallas_call(
        lambda *refs: choose_kernel(receivers, len(flat), *refs),
        name="choose",
        out_shape=[shape] * receivers,
        in_specs=[pl.BlockSpec(memory_space=pltpu.SMEM)]
        + [pl.BlockSpec(memory_space=pl.ANY)] * len(flat),
        out_specs=[pl.BlockSpec(memory_space=pltpu.VMEM)] * receivers,
        scratch_shapes=[
            pltpu.VMEM((PARTS, len(flat) // PARTS) + flat[0].shape, flat[0].dtype),
            pltpu.SemaphoreType.DMA((len(flat),)),
        ],
    )(picks, *flat)


def tiles_kernel(based, rows, *refs):
    arrived, (out, columns) = refs[based:-2], refs[-2:]
    _, halves, parts, depth, _ = arrived[0].shape

    @pl.when(pl.program_id(1) == 0)
    def _():
        slot = pl.program_id(0)
        at = 0
        for block in arrived:
            for z_half in range(halves):
                for part in range(parts):
                    columns[at : at + depth, :] = block[slot, z_half, part]
                    at += depth

    result = dot(rows[...], columns[...])
    out[0] = result + refs[0][0] if based else result


def tiles(rows, arrived, offset, base=None):
    height = rows.shape[0]
    slots, halves, parts, piece, points = arrived[0].shape
    depth = len(arrived) * halves * parts * piece
    step = height // 5
    whole = pl.BlockSpec(arrived[0].shape, lambda s, m: (0,) * 5)
    tile = pl.BlockSpec((1, step, points), lambda s, m: (s, m, 0))
    bases = [] if base is None else [base]
    return pl.pallas_call(
        lambda *refs: tiles_kernel(len(bases), *refs),
        name="tiles",
        grid=(slots, height // step),
        out_shape=jax.ShapeDtypeStruct((slots, height, points), jnp.float32),
        in_specs=[pl.BlockSpec((step, depth), lambda s, m: (m, offset))]
        + [tile] * len(bases)
        + [whole] * len(arrived),
        out_specs=tile,
        scratch_shapes=[pltpu.VMEM((depth, points), rows.dtype)],
        compiler_params=pltpu.CompilerParams(vmem_limit_bytes=40 << 20),
    )(rows, *bases, *arrived)


def per_device(orbitals, val_energy, cond_energy, pair_index, sphere_points, tile_offsets):
    fft_devices = lax.axis_size("fft")
    pair_groups = lax.axis_size("pairs")
    planes = orbitals.shape[1]
    length_one = planes * fft_devices
    length_two = orbitals.shape[2]
    length_three = orbitals.shape[3] // 2
    valence_count = val_energy.shape[0]
    cond_count = cond_energy.shape[0]
    group_pairs = pair_index.shape[0]
    all_pairs = group_pairs * pair_groups
    block_size = sphere_points.shape[0]
    column_count = COLS_ALL // fft_devices
    plane_size = length_two * length_three
    grid_total = length_one * plane_size
    half = group_pairs // CORES

    fft_place = lax.axis_index("fft")
    pair_place = lax.axis_index("pairs")
    core = fft_place % CORES
    z_low = fft_place // CORES % ZL
    z_high = pair_place % 2
    z_place = z_high * ZL + z_low
    y_place = pair_place // 2

    my_list = sphere_points[:column_count]
    spread_list = jnp.broadcast_to(my_list[None], (fft_devices, column_count))
    lists = lax.all_to_all(spread_list, "fft", 0, 0, tiled=True).reshape(-1)
    own_offsets = tile_offsets[0]
    other_offsets = fetch(own_offsets, dcore=1)

    valence = pair_index // cond_count
    conduction = pair_index % cond_count
    packed = front(orbitals, valence, valence_count + conduction, lists, fft_devices)
    data = lax.all_to_all(packed, "fft", split_axis=0, concat_axis=0, tiled=True)

    energy_gap = jnp.take(cond_energy, conduction, mode="clip") - jnp.take(
        val_energy, valence, mode="clip"
    )
    scale = jnp.sqrt(2.0 / (energy_gap * math.sqrt(all_pairs))) / math.sqrt(grid_total)
    mine, other = points(core, data, sphere_points, my_list, scale, length_one, plane_size)
    quarter = half // PARTS
    first_core = core == 0
    swapped = fetch(other, dcore=1)
    chip = jnp.where(first_core, jnp.stack([mine, swapped], 1), jnp.stack([swapped, mine], 1))

    steps = jnp.arange(Y, dtype=jnp.int32)
    receivers_y = (y_place - steps) % Y
    slot = 4 * receivers_y[:, None] + 2 * z_high + jnp.arange(2, dtype=jnp.int32)[None, :]
    picks = []
    for dcore in range(CORES):
        offsets = own_offsets if dcore == 0 else other_offsets
        receiver_core = core ^ dcore
        place = z_low * CORES + receiver_core + jnp.take(offsets, slot, mode="clip")
        slab_index = place // (ZL * CORES)
        inside = place % (ZL * CORES)
        z_wanted = inside[..., None] // CORES + ZL * jnp.arange(2, dtype=jnp.int32)
        ring_index = (z_wanted - z_place) % Z
        picks.append((ring_index * 3 + slab_index[..., None]) * CORES + inside[..., None] % CORES)
    picks = jnp.stack(picks, 1).reshape(-1)

    rings = []
    for part in range(PARTS):
        own = chip[part]
        slabs = jnp.concatenate([own, fetch(own, dx=1), fetch(own, dx=2)])
        ring = {0: slabs}
        last = Z // 2
        for step in range(1, last):
            ring[step] = fetch(ring[step - 1], dz=1)
            ring[-step] = fetch(ring[1 - step], dz=-1)
        if part % 2 == 0:
            ring[last] = fetch(ring[last - 1], dz=1)
        else:
            ring[last] = fetch(ring[1 - last], dz=-1)
        rings.append([ring[step if step <= last else step - Z] for step in range(Z)])
    own_rows = after(jnp.stack([mine, other]), rings[0][1])
    far_rows = fetch(own_rows, dz=ZL)
    lower = z_high == 0
    row_part = jnp.stack(
        [jnp.where(lower, own_rows, far_rows), jnp.where(lower, far_rows, own_rows)], 1
    )
    row_parts = [row_part] + [fetch(row_part, dy=dy) for dy in range(1, Y)]

    chosen = choose(picks, rings, Y * CORES)
    arrived = {}
    for dy in (1, 2, 3, 0):
        for dcore in range(CORES):
            piece = chosen[dy * CORES + dcore].reshape(2, 2, PARTS, 2 * quarter, block_size)
            arrived[dy, dcore] = fetch(piece, dy=dy, dcore=dcore) if dy + dcore else piece
    arrived = [arrived[key] for key in sorted(arrived)]

    rows = jnp.stack(row_parts)
    rows = rows.reshape(-1, 2, quarter, block_size)
    turned = jnp.stack([-rows[:, 1], rows[:, 0]], 1).reshape(-1, block_size)
    both = jnp.concatenate([-rows.reshape(-1, block_size), turned], 1).T
    early = tiles(both, arrived[: Y * CORES // 2], 0)
    late = tiles(both, arrived[Y * CORES // 2 :], 1, early)
    return late.reshape(1, 2, 2, block_size, block_size)


def solution(mesh):
    placed = (P(None, "fft", None, None), P(), P(), P("pairs"), P("fft"), P("fft", None))
    return jax.shard_map(
        per_device,
        mesh=mesh,
        in_specs=placed,
        out_specs=P("fft", "pairs", None, None, None),
        check_vma=False,
    )
```
